32 devices in a mesh: cls: 2 (over core), img: 16 (over z, y, x).
Axes of the slice: x: 2, y: 2, z: 4, core: 2. Of those that a mesh axis runs over, the one named last changes fastest.
Arguments:
- images: bfloat16 [1792, 7200], P(('cls', 'img')), may hold values from -8 to 8
- projections: bfloat16 [256, 7200], P('cls'), may hold values from -0.42426407 to 0.42426407
- noise_power: float32 [32, 7200], replicated, may hold values from 0.5 to 4
- class_logprior: float32 [4], replicated, may hold values from -1.5 to 1.5
- groups: int32 [1792], P(('cls', 'img')), may hold values from 0 to 31
- offsets: int32 [1792], P(('cls', 'img')), may hold values from 0 to 3
Outputs:
- weighted_sums: float32 [256, 7200], P(('cls', 'img'))
- log_evidence: float32 [1792], P(('cls', 'img'))
The draws below stay inside these ranges and needn't reach their ends.
All inputs are finite; a program needn't handle non-finite values.
Results may differ from the reference program's by a relative error of at most 0.0064.
Values may be sent and summed in bfloat16 or wider, within the bound.
No kernel may reach another device: no remote copies, remote signals or barrier semaphores. Data moves between devices by JAX's collectives and lax.ppermute only.
A program may use at most 64 MiB of HBM per device.

```python
import math
import jax
import jax.numpy as jnp
from jax import lax

F = 7200
CLASSES = 4
GROUPS = 32
IMG_DEV = 56
PROJS = 256
IMAGES = 1792
N_CLS = 2


aligned_pairs = 8


mean_inverse = 1.75 / math.log(8.0)


def shared_layout(key):
    layout_key = jax.random.fold_in(key, 911)
    pair_order = jax.random.permutation(jax.random.fold_in(layout_key, 1), PROJS // 2)
    image_order = jax.random.permutation(jax.random.fold_in(layout_key, 2), IMAGES)
    first_rows = 2 * pair_order[:aligned_pairs]
    return (first_rows, first_rows + 1, image_order[:aligned_pairs])


def base_rows(key):
    base_key = jax.random.fold_in(key, 913)
    values = jnp.clip(jax.random.normal(base_key, (PROJS, F), jnp.float32), -6.0, 6.0)
    return values


def drawn_base(key):
    return jax.random.uniform(jax.random.fold_in(key, 917), (aligned_pairs, F), jnp.float32, -math.sqrt(3.0), math.sqrt(3.0))


def targets():
    return 200.0 + 60.0 * (jnp.arange(aligned_pairs) % 4).astype(jnp.float32)


def projection_level():
    return 18.0 / math.sqrt(F)


def image_level():
    level = projection_level()
    return (targets() + 0.5 * level * level * F * mean_inverse) / (level * F * mean_inverse)


def draw_projections(key, part):
    values = base_rows(key)
    row_scale = jnp.exp(jax.random.uniform(jax.random.fold_in(key, 914), (PROJS,), jnp.float32, math.log(0.5), math.log(2.0)))
    result = 3.0 * row_scale[:, None] * values / math.sqrt(F)
    first_rows, second_rows, image_rows = shared_layout(key)
    shared = drawn_base(key)
    level = projection_level()
    half_quadratic = 0.5 * level * level * F * mean_inverse
    epsilon = 2.0 / (targets() - half_quadratic)
    result = result.at[first_rows].set(level * shared)
    result = result.at[second_rows].set(level * (1.0 - epsilon)[:, None] * shared)
    return result.astype(jnp.bfloat16)


def draw_images(key, part):
    image_key = jax.random.fold_in(key, 915)
    values = jnp.clip(jax.random.normal(image_key, (IMAGES, F), jnp.float32), -6.0, 6.0)
    first_rows, second_rows, image_rows = shared_layout(key)
    shared = drawn_base(key)
    values = values.at[image_rows].set(image_level()[:, None] * shared)
    return values.astype(jnp.bfloat16)


def touch_ends(values, stream_key, smallest, high):
    spot = [jax.random.randint(jax.random.fold_in(stream_key, axis), (), 0, length) for axis, length in enumerate(values.shape)]
    longest = values.shape.index(max(values.shape))
    next_to = spot[:longest] + [(spot[longest] + 1) % values.shape[longest]] + spot[longest + 1:]
    return values.at[tuple(spot)].set(smallest).at[tuple(next_to)].set(high)


def setup_inputs(seed: int = 0) -> dict:
    keys = jax.random.split(jax.random.key(seed), 7)
    images = draw_images(jax.random.fold_in(keys[6], 71), 0)
    projections = draw_projections(jax.random.fold_in(keys[6], 71), 0)
    noise_power = jnp.clip(jnp.exp(jax.random.uniform(keys[2], (GROUPS, F), jnp.float32, math.log(0.5), math.log(4.0))), 0.5, 4.0)
    class_logprior = jnp.clip(jax.random.uniform(keys[3], (CLASSES,), jnp.float32, -1.5, 1.5), -1.5, 1.5)
    groups = touch_ends(jax.random.randint(keys[4], (IMAGES,), 0, GROUPS), jax.random.fold_in(keys[4], 1), 0, GROUPS - 1).astype(jnp.int32)
    offsets = touch_ends(jax.random.randint(keys[5], (IMAGES,), 0, CLASSES), jax.random.fold_in(keys[5], 1), 0, CLASSES - 1).astype(jnp.int32)
    return {"images": images, "projections": projections, "noise_power": noise_power, "class_logprior": class_logprior, "groups": groups, "offsets": offsets}


def reference(images, projections, noise_power, class_logprior, groups, offsets):
    inverse = 1.0 / noise_power
    whitened = (images.astype(jnp.float32) * inverse[groups]).astype(jnp.bfloat16)
    proj_float = projections.astype(jnp.float32)
    quadratic = jnp.dot(inverse, (proj_float * proj_float).T, precision=lax.Precision.HIGHEST)
    per_class = PROJS // CLASSES
    class_of = jnp.arange(PROJS, dtype=jnp.int32) // per_class
    class_shift = (class_of[None, :] - jnp.arange(CLASSES, dtype=jnp.int32)[:, None]) % CLASSES
    prior_table = class_logprior[class_shift]
    block_rows = IMG_DEV * N_CLS
    blocks = IMAGES // block_rows
    white_blocks = whitened.reshape(blocks, block_rows, F)
    group_blocks = groups.reshape(blocks, block_rows)
    offset_blocks = offsets.reshape(blocks, block_rows)

    def one_block(summed, inputs):
        batch_rows, group_ids, offset_ids = inputs
        scores = jnp.dot(batch_rows, projections.T, preferred_element_type=jnp.float32)
        scores = scores + (-0.5 * quadratic[group_ids] + prior_table[offset_ids])
        peak = jnp.max(scores, axis=1)
        evidence = peak + jnp.log(jnp.sum(jnp.exp(scores - peak[:, None]), axis=1))
        posterior = jnp.exp(scores - evidence[:, None]).astype(jnp.bfloat16)
        summed = summed + jnp.einsum("bp,bf->pf", posterior.astype(jnp.float32), batch_rows.astype(jnp.float32))
        return summed, evidence

    start_sums = jnp.zeros((PROJS, F), jnp.float32)
    weighted_sums, evidence = lax.scan(one_block, start_sums, (white_blocks, group_blocks, offset_blocks))
    return weighted_sums, evidence.reshape(IMAGES)
```

```python
import jax
import jax.numpy as jnp
from jax import lax
from jax.sharding import PartitionSpec as P

LANES = 128


def group_of(members):
    return next(size for size in (4, 2, 1) if members % size == 0)


def shifted(value, axis, step):
    count = lax.axis_size(axis)
    return lax.ppermute(value, axis, [(place, (place + step) % count) for place in range(count)])


def crossed(value, axis, flip):
    count = lax.axis_size(axis)
    return lax.ppermute(value, axis, [(place, place ^ flip) for place in range(count)])


def gathered_from(value, axis):
    return [value] + [shifted(value, axis, step) for step in range(1, lax.axis_size(axis))]


def body(images, projections, noise_power, class_logprior, groups, offsets):
    rows_here, terms = images.shape
    proj_here = projections.shape[0]
    cycle_size = lax.axis_size("cls")
    cycle_place = lax.axis_index("cls")
    owners = lax.axis_size("img")
    team = group_of(owners)
    member = lax.axis_index("img") % team
    width = -(-terms // (LANES * team)) * LANES
    group_count = noise_power.shape[0]
    class_count = class_logprior.shape[0]
    inverse = 1.0 / noise_power
    group_hot = (groups[:, None] == jnp.arange(group_count, dtype=jnp.int32)[None, :]).astype(
        jnp.float32
    )
    offset_hot = (offsets[:, None] == jnp.arange(class_count, dtype=jnp.int32)[None, :]).astype(
        jnp.float32
    )
    row_inverse = jnp.dot(group_hot, inverse, precision=lax.Precision.HIGHEST)
    whitened = (images.astype(jnp.float32) * row_inverse).astype(jnp.bfloat16)
    tag_rows = jnp.concatenate([group_hot, offset_hot], axis=1).astype(jnp.bfloat16)

    gathered = jnp.concatenate(gathered_from(whitened, "cls"), axis=0)
    labels = jnp.concatenate(gathered_from(tag_rows, "cls"), axis=0)
    padded = jnp.pad(whitened, ((0, 0), (0, width * team - terms)))
    parts = [
        lax.dynamic_slice_in_dim(padded, (member ^ flip) * width, width, axis=1)
        for flip in range(team)
    ]
    slab_own = jnp.concatenate(
        [parts[0]] + [crossed(parts[flip], "img", flip) for flip in range(1, team)], axis=0
    )
    slabs = gathered_from(slab_own, "cls")

    proj_float = projections.astype(jnp.float32)
    quadratic = jnp.dot(inverse, (proj_float * proj_float).T, precision=lax.Precision.HIGHEST)
    global_index = cycle_place * proj_here + jnp.arange(proj_here, dtype=jnp.int32)
    per_class = proj_here * cycle_size // class_count
    class_of = global_index // per_class
    class_shift = (
        class_of[None, :] - jnp.arange(class_count, dtype=jnp.int32)[:, None]
    ) % class_count
    matches = class_shift[:, :, None] == jnp.arange(class_count, dtype=jnp.int32)[None, None, :]
    prior_table = jnp.sum(jnp.where(matches, class_logprior[None, None, :], 0.0), axis=2)
    bias_table = jnp.concatenate([-0.5 * quadratic, prior_table], axis=0)
    products = jnp.einsum("bf,pf->bp", gathered, projections, preferred_element_type=jnp.float32)
    scores = products + jnp.dot(
        labels.astype(jnp.float32), bias_table, precision=lax.Precision.HIGHEST
    )
    local_peak = jnp.max(scores, axis=1)
    local_sum = jnp.sum(jnp.exp(scores - local_peak[:, None]), axis=1)
    stats = jnp.stack([local_peak, local_sum]).reshape(2, cycle_size, rows_here)
    peak, exp_sum = stats[0], stats[1]
    for step in range(1, cycle_size):
        turned = jnp.roll(stats, step, axis=1)
        other = shifted(turned, "cls", step)
        top = jnp.maximum(peak, other[0])
        exp_sum = exp_sum * jnp.exp(peak - top) + other[1] * jnp.exp(other[0] - top)
        peak = top
    evidence = (peak + jnp.log(exp_sum)).reshape(cycle_size * rows_here)
    posterior = jnp.exp(scores - evidence[:, None]).astype(jnp.bfloat16)
    weights = posterior[None]
    flip = 1
    while flip < team:
        weights = jnp.concatenate([weights, crossed(weights, "img", flip)], axis=0)
        flip *= 2
    weights = weights.reshape(team, cycle_size, rows_here, proj_here)
    sums = sum(
        jnp.einsum(
            "bp,bf->pf",
            weights[:, place].reshape(team * rows_here, proj_here),
            slabs[place],
            preferred_element_type=jnp.float32,
        )
        for place in range(cycle_size)
    )
    blocks = sums.astype(jnp.bfloat16).reshape(owners, proj_here // owners, width)
    pieces = lax.all_to_all(blocks, "img", 0, 0)
    pieces = pieces.reshape(owners // team, team, proj_here // owners, width)
    total = jnp.sum(pieces.astype(jnp.float32), axis=0)
    sum_rows = jnp.concatenate([total[place] for place in range(team)], axis=1)[:, :terms]
    return (sum_rows, evidence[:rows_here])


def solution(mesh):
    in_specs = (
        P(("cls", "img"), None),
        P("cls", None),
        P(),
        P(),
        P(("cls", "img")),
        P(("cls", "img")),
    )
    out_specs = (P(("cls", "img"), None), P(("cls", "img")))
    return jax.shard_map(body, mesh=mesh, in_specs=in_specs, out_specs=out_specs, check_vma=False)
```

```python
import functools

import jax
import jax.numpy as jnp
from jax import lax
from jax.experimental import pallas as pl
from jax.experimental.pallas import tpu as pltpu
from jax.sharding import PartitionSpec as P

LANES = 128
PARTS = 3
GRANT = 24 * 2**20


def group_of(members):
    return next(size for size in (4, 2, 1) if members % size == 0)


def shifted(value, axis, step):
    count = lax.axis_size(axis)
    return lax.ppermute(value, axis, [(place, (place + step) % count) for place in range(count)])


def crossed(value, axis, flip):
    count = lax.axis_size(axis)
    return lax.ppermute(value, axis, [(place, place ^ flip) for place in range(count)])


def gathered_from(value, axis):
    return [value] + [shifted(value, axis, step) for step in range(1, lax.axis_size(axis))]


def split(value, count):
    pieces = []
    for _ in range(count):
        piece = value.astype(jnp.bfloat16)
        pieces.append(piece)
        value = value - piece.astype(jnp.float32)
    return pieces


def first_rows(left, right):
    return lax.dot_general(left, right, (((0,), (0,)), ((), ())), preferred_element_type=jnp.float32)


def column_of(shape, start):
    return start + lax.broadcasted_iota(jnp.int32, shape, 1)


def whiten_kernel(terms, tag_column, groups_ref, offsets_ref, images_ref, noise_ref, out_ref, *, classes):
    step = pl.program_id(0)
    rows, width = out_ref.shape
    group_count = noise_ref.shape[0]

    def hot(ids, count):
        places = lax.broadcasted_iota(jnp.int32, (count, rows), 0)
        return jnp.where(places == ids, 1.0, 0.0)

    group_hot = hot(groups_ref[...], group_count).astype(jnp.bfloat16)
    pieces = split(1.0 / noise_ref[...], PARTS)
    row_inverse = first_rows(
        jnp.concatenate([group_hot] * PARTS, axis=0), jnp.concatenate(pieces, axis=0)
    )
    white = images_ref[...].astype(jnp.float32) * row_inverse
    last = pl.num_programs(0) - 1

    @pl.when(step != last)
    def _():
        out_ref[...] = white.astype(jnp.bfloat16)

    @pl.when(step == last)
    def _():
        start = last * width
        kept = jnp.where(column_of((rows, width), start) < terms, white, 0.0)
        out_ref[...] = kept.astype(jnp.bfloat16)
        tile = tag_column // LANES * LANES
        for ids, count, shift in (
            (groups_ref[...], group_count, tag_column - tile),
            (offsets_ref[...], classes, tag_column - tile + group_count),
        ):
            tall = -(-count // 16) * 16
            line = lax.broadcasted_iota(jnp.int32, (tall, LANES), 0)
            lane = lax.broadcasted_iota(jnp.int32, (tall, LANES), 1)
            spread = jnp.where(lane == line + shift, 1.0, 0.0).astype(jnp.bfloat16)
            mark = first_rows(hot(ids, tall).astype(jnp.bfloat16), spread)
            place = pl.ds(tile - start, LANES)
            out_ref[:, place] = out_ref[:, place] + mark.astype(jnp.bfloat16)


def table_kernel(shift, per_class, place_ref, prior_ref, noise_ref, tall_ref, out_ref):
    group_count = noise_ref.shape[0]
    proj_here = tall_ref.shape[1]
    class_count = prior_ref.shape[0]
    tall = tall_ref[...].astype(jnp.float32)
    high, low = split(tall * tall, 2)
    narrow = jnp.concatenate(split(1.0 / noise_ref[...], 2), axis=0)
    both = jnp.dot(narrow, high, preferred_element_type=jnp.float32) + jnp.dot(
        narrow, low, preferred_element_type=jnp.float32
    )
    out_ref[...] = jnp.zeros_like(out_ref)
    out_ref[pl.ds(shift, group_count), :] = -0.5 * (both[:group_count] + both[group_count:])
    index = place_ref[0] * proj_here + lax.broadcasted_iota(jnp.int32, (1, proj_here), 1)
    class_of = jnp.zeros_like(index)
    for bound in range(1, class_count):
        class_of = class_of + jnp.where(index >= bound * per_class, 1, 0)
    for offset in range(class_count):
        away = class_of - offset
        away = jnp.where(away < 0, away + class_count, away)
        row = jnp.zeros((1, proj_here), jnp.float32)
        for distance in range(class_count):
            row = jnp.where(away == distance, prior_ref[distance], row)
        out_ref[pl.ds(shift + group_count + offset, 1), :] = row


def score_kernel(tag_column, count, *refs):
    white_refs = refs[:count]
    tall_ref, table_ref, scores_ref, stats_ref = refs[count:]
    terms, proj_here = tall_ref.shape
    tile = tag_column // LANES * LANES
    rows = jnp.concatenate([ref[:, :tile] for ref in white_refs], axis=0)
    marks = jnp.concatenate([ref[:, tile : tile + LANES] for ref in white_refs], axis=0)
    high, *rest = split(table_ref[...], PARTS)
    if tile < terms:
        high = jnp.concatenate([tall_ref[tile:, :], high[terms - tile :]], axis=0)
    scores = jnp.dot(rows, tall_ref[:tile, :], preferred_element_type=jnp.float32)
    bias = sum(jnp.dot(marks, piece, preferred_element_type=jnp.float32) for piece in rest)
    scores = scores + (jnp.dot(marks, high, preferred_element_type=jnp.float32) + bias)
    peak = jnp.max(scores, axis=1, keepdims=True)
    weight = jnp.sum(jnp.exp(scores - peak), axis=1, keepdims=True)
    scores_ref[...] = scores
    lane = lax.broadcasted_iota(jnp.int32, stats_ref.shape, 1)
    stats_ref[...] = jnp.where(lane == 0, peak, weight)


def posterior_kernel(count, rows_here, *refs):
    scores_ref = refs[0]
    stats_refs = refs[1 : 1 + count]
    posterior_ref, evidence_ref = refs[1 + count :]
    for place in range(count):
        mine = pl.ds(place * rows_here, rows_here)
        peak = stats_refs[0][mine, 0:1]
        weight = stats_refs[0][mine, 1:2]
        for step in range(1, count):
            theirs = pl.ds((place - step) % count * rows_here, rows_here)
            other_peak = stats_refs[step][theirs, 0:1]
            other_weight = stats_refs[step][theirs, 1:2]
            top = jnp.maximum(peak, other_peak)
            weight = weight * jnp.exp(peak - top) + other_weight * jnp.exp(other_peak - top)
            peak = top
        evidence = peak + jnp.log(weight)
        posterior_ref[mine, :] = jnp.exp(scores_ref[mine, :] - evidence).astype(jnp.bfloat16)
        if place == 0:
            evidence_ref[...] = jnp.broadcast_to(evidence, evidence_ref.shape)


def sums_kernel(team, count, *refs):
    weight_refs, slab_refs, out_ref = refs[:team], refs[team:-1], refs[-1]
    rows_here = weight_refs[0].shape[0] // count
    weights = [
        ref[pl.ds(place * rows_here, rows_here), :]
        for place in range(count)
        for ref in weight_refs
    ]
    slabs = [ref[...] for ref in slab_refs]
    out_ref[...] = first_rows(
        jnp.concatenate(weights, axis=0), jnp.concatenate(slabs, axis=0)
    ).astype(out_ref.dtype)


def body(images, projections, noise_power, class_logprior, groups, offsets):
    rows_here, terms = images.shape
    proj_here = projections.shape[0]
    cycle_size = lax.axis_size("cls")
    cycle_place = lax.axis_index("cls")
    owners = lax.axis_size("img")
    team = group_of(owners)
    member = lax.axis_index("img") % team
    group_count = noise_power.shape[0]
    class_count = class_logprior.shape[0]
    tags = group_count + class_count
    tag_column = terms if terms % LANES + tags <= LANES else -(-terms // LANES) * LANES
    width = -(-(tag_column + tags) // (LANES * team)) * LANES
    per_class = proj_here * cycle_size // class_count
    all_rows = cycle_size * rows_here
    columns = functools.partial(pl.BlockSpec, index_map=lambda j: (0, j))
    still = functools.partial(pl.BlockSpec, index_map=lambda j: (0, 0))
    grant = functools.partial(pltpu.CompilerParams, vmem_limit_bytes=GRANT)
    scalars = pl.BlockSpec(memory_space=pltpu.SMEM)
    local = pl.BlockSpec(memory_space=pltpu.VMEM)

    whitened = pl.pallas_call(
        functools.partial(whiten_kernel, terms, tag_column, classes=class_count),
        out_shape=jax.ShapeDtypeStruct((rows_here, team * width), jnp.bfloat16),
        grid=(team,),
        in_specs=[
            still((1, rows_here)),
            still((1, rows_here)),
            columns((rows_here, width)),
            columns((group_count, width)),
        ],
        out_specs=columns((rows_here, width)),
        compiler_params=grant(dimension_semantics=("arbitrary",)),
        cost_estimate=pl.CostEstimate(
            flops=2 * rows_here * PARTS * group_count * terms,
            bytes_accessed=4 * rows_here * terms + 4 * group_count * terms,
            transcendentals=0,
        ),
        name="whiten",
    )(groups.reshape(1, rows_here), offsets.reshape(1, rows_here), images, noise_power)

    tall = projections.T
    table = pl.pallas_call(
        functools.partial(table_kernel, tag_column % LANES, per_class),
        out_shape=jax.ShapeDtypeStruct((LANES, proj_here), jnp.float32),
        in_specs=[scalars, scalars, local, local],
        out_specs=local,
        cost_estimate=pl.CostEstimate(
            flops=8 * proj_here * group_count * terms,
            bytes_accessed=2 * proj_here * terms + 4 * group_count * terms,
            transcendentals=0,
        ),
        compiler_params=grant(),
        name="table",
    )(cycle_place.reshape(1), class_logprior, noise_power, tall)

    gathered = gathered_from(whitened, "cls")
    parts = [
        lax.dynamic_slice_in_dim(whitened, (member ^ flip) * width, width, axis=1)
        for flip in range(team)
    ]
    swapped = [parts[0]] + [crossed(parts[flip], "img", flip) for flip in range(1, team)]

    scores, stats = pl.pallas_call(
        functools.partial(score_kernel, tag_column, cycle_size),
        out_shape=(
            jax.ShapeDtypeStruct((all_rows, proj_here), jnp.float32),
            jax.ShapeDtypeStruct((all_rows, LANES), jnp.float32),
        ),
        in_specs=[local] * (cycle_size + 2),
        out_specs=(local, local),
        cost_estimate=pl.CostEstimate(
            flops=2 * all_rows * proj_here * terms,
            bytes_accessed=2 * (all_rows + proj_here) * terms,
            transcendentals=all_rows * proj_here,
        ),
        compiler_params=grant(),
        name="scores",
    )(*gathered, tall, table)

    posterior, evidence = pl.pallas_call(
        functools.partial(posterior_kernel, cycle_size, rows_here),
        out_shape=(
            jax.ShapeDtypeStruct((all_rows, proj_here), jnp.bfloat16),
            jax.ShapeDtypeStruct((rows_here, LANES), jnp.float32),
        ),
        in_specs=[local] * (cycle_size + 1),
        out_specs=(local, local),
        compiler_params=grant(),
        name="posterior",
    )(scores, *gathered_from(stats, "cls"))

    weights = [posterior] + [crossed(posterior, "img", flip) for flip in range(1, team)]
    swapped, _ = lax.optimization_barrier((swapped, posterior))
    arrived = jnp.concatenate(swapped[1:], axis=0)
    slabs = [swapped[0], arrived]
    for step in range(1, cycle_size):
        slabs.append(lax.dynamic_slice_in_dim(gathered[step], member * width, width, axis=1))
        slabs.append(shifted(arrived, "cls", step))
    sums = pl.pallas_call(
        functools.partial(sums_kernel, team, cycle_size),
        out_shape=jax.ShapeDtypeStruct((proj_here, width), jnp.bfloat16),
        in_specs=[local] * (team + 2 * cycle_size),
        out_specs=local,
        cost_estimate=pl.CostEstimate(
            flops=2 * team * all_rows * proj_here * width,
            bytes_accessed=2 * (team * all_rows + proj_here) * width,
            transcendentals=0,
        ),
        compiler_params=grant(),
        name="sums",
    )(*weights, *slabs)
    blocks = sums.reshape(owners, proj_here // owners, width)
    pieces = lax.all_to_all(blocks, "img", 0, 0)
    pieces = pieces.reshape(owners // team, team, proj_here // owners, width)
    total = jnp.sum(pieces.astype(jnp.float32), axis=0)
    sum_rows = jnp.concatenate([total[place] for place in range(team)], axis=1)[:, :terms]
    return (sum_rows, evidence[:, 0])


def solution(mesh):
    in_specs = (
        P(("cls", "img"), None),
        P("cls", None),
        P(),
        P(),
        P(("cls", "img")),
        P(("cls", "img")),
    )
    out_specs = (P(("cls", "img"), None), P(("cls", "img")))
    return jax.shard_map(body, mesh=mesh, in_specs=in_specs, out_specs=out_specs, check_vma=False)
```

```python
import functools

import jax
import jax.numpy as jnp
from jax import lax
from jax.experimental import pallas as pl
from jax.experimental.pallas import tpu as pltpu
from jax.sharding import PartitionSpec as P


LANES = 128
PARTS = 3
GRANT = 24 * 2**20


def group_of(members):
    return next(size for size in (4, 2, 1) if members % size == 0)


def shifted(value, axis, step):
    count = lax.axis_size(axis)
    return lax.ppermute(value, axis, [(place, (place + step) % count) for place in range(count)])


def crossed(value, axis, flip):
    count = lax.axis_size(axis)
    return lax.ppermute(value, axis, [(place, place ^ flip) for place in range(count)])


def gathered_from(value, axis):
    return [value] + [shifted(value, axis, step) for step in range(1, lax.axis_size(axis))]


def split(value, count):
    pieces = []
    for _ in range(count):
        piece = value.astype(jnp.bfloat16)
        pieces.append(piece)
        value = value - piece.astype(jnp.float32)
    return pieces


def first_rows(left, right):
    return lax.dot_general(left, right, (((0,), (0,)), ((), ())), preferred_element_type=jnp.float32)


def whiten_kernel(
    team,
    tag_column,
    classes,
    groups_hbm,
    offsets_hbm,
    images_hbm,
    noise_hbm,
    tall_hbm,
    white_ref,
    narrow_ref,
    tall_ref,
    *rest,
):
    part_refs = rest[:team]
    groups_ref, offsets_ref, images_ref, noise_ref, *sems = rest[team:]
    small_sems, image_sems, noise_sems, tall_sem = sems
    rows, terms = images_ref.shape
    width = white_ref.shape[1] // team
    group_count = noise_ref.shape[0]
    spans = [(place * width, min(terms, (place + 1) * width)) for place in range(team)]
    small = [
        pltpu.make_async_copy(groups_hbm, groups_ref, small_sems.at[0]),
        pltpu.make_async_copy(offsets_hbm, offsets_ref, small_sems.at[1]),
    ]
    for copy in small:
        copy.start()
    large = []
    for place, (low, high) in enumerate(spans):
        cut = pl.ds(low, high - low)
        pair = (
            pltpu.make_async_copy(noise_hbm.at[:, cut], noise_ref.at[:, cut], noise_sems.at[place]),
            pltpu.make_async_copy(images_hbm.at[:, cut], images_ref.at[:, cut], image_sems.at[place]),
        )
        for copy in pair:
            copy.start()
        large.append(pair)
    tall_copy = pltpu.make_async_copy(tall_hbm, tall_ref, tall_sem)
    tall_copy.start()

    def hot(ids, count):
        places = lax.broadcasted_iota(jnp.int32, (count, rows), 0)
        return jnp.where(places == ids, 1.0, 0.0)

    for copy in small:
        copy.wait()
    group_hot = hot(groups_ref[...], group_count).astype(jnp.bfloat16)
    chooser = jnp.concatenate([group_hot] * PARTS, axis=0)
    member = lax.rem(lax.axis_index("img"), team)
    for place, (low, high) in enumerate(spans):
        noise_copy, image_copy = large[place]
        noise_copy.wait()
        pieces = split(1.0 / noise_ref[:, low:high], PARTS)
        narrow_ref[:group_count, low:high] = pieces[0]
        narrow_ref[group_count:, low:high] = pieces[1]
        row_inverse = first_rows(chooser, jnp.concatenate(pieces, axis=0))
        image_copy.wait()
        white = images_ref[:, low:high].astype(jnp.float32) * row_inverse
        missing = width - (high - low)
        if missing:
            white = jnp.concatenate([white, jnp.zeros((rows, missing), jnp.float32)], axis=1)
            tile = tag_column // LANES * LANES
            mark = jnp.zeros((rows, LANES), jnp.float32)
            for ids, count, shift in (
                (groups_ref[...], group_count, tag_column - tile),
                (offsets_ref[...], classes, tag_column - tile + group_count),
            ):
                tall = -(-count // 16) * 16
                line = lax.broadcasted_iota(jnp.int32, (tall, LANES), 0)
                lane = lax.broadcasted_iota(jnp.int32, (tall, LANES), 1)
                spread = jnp.where(lane == line + shift, 1.0, 0.0).astype(jnp.bfloat16)
                mark = mark + first_rows(hot(ids, tall).astype(jnp.bfloat16), spread)
            edge = tile - place * width
            white = jnp.concatenate(
                [white[:, :edge], white[:, edge : edge + LANES] + mark, white[:, edge + LANES :]],
                axis=1,
            )
        white = white.astype(jnp.bfloat16)
        white_ref[:, place * width : (place + 1) * width] = white
        for flip, part_ref in enumerate(part_refs):

            @pl.when(member == place ^ flip)
            def _():
                part_ref[...] = white

    tall_copy.wait()


def table_kernel(shift, per_class, prior_ref, narrow_ref, tall_ref, out_ref):
    group_count = narrow_ref.shape[0] // 2
    proj_here = tall_ref.shape[1]
    class_count = prior_ref.shape[0]
    tall = tall_ref[...].astype(jnp.float32)
    high, low = split(tall * tall, 2)
    narrow = narrow_ref[...]
    both = jnp.dot(narrow, high, preferred_element_type=jnp.float32) + jnp.dot(
        narrow, low, preferred_element_type=jnp.float32
    )
    out_ref[...] = jnp.zeros_like(out_ref)
    out_ref[pl.ds(shift, group_count), :] = -0.5 * (both[:group_count] + both[group_count:])
    index = lax.axis_index("cls") * proj_here + lax.broadcasted_iota(jnp.int32, (1, proj_here), 1)
    class_of = jnp.zeros_like(index)
    for bound in range(1, class_count):
        class_of = class_of + jnp.where(index >= bound * per_class, 1, 0)
    for offset in range(class_count):
        away = class_of - offset
        away = jnp.where(away < 0, away + class_count, away)
        row = jnp.zeros((1, proj_here), jnp.float32)
        for distance in range(class_count):
            row = jnp.where(away == distance, prior_ref[distance], row)
        out_ref[pl.ds(shift + group_count + offset, 1), :] = row


def score_kernel(tag_column, count, *refs):
    white_refs = refs[:count]
    tall_ref, table_ref, scores_ref, stats_ref = refs[count:]
    terms, _ = tall_ref.shape
    tile = tag_column // LANES * LANES
    rows = jnp.concatenate([ref[:, :tile] for ref in white_refs], axis=0)
    marks = jnp.concatenate([ref[:, tile : tile + LANES] for ref in white_refs], axis=0)
    high, *rest = split(table_ref[...], PARTS)
    if tile < terms:
        high = jnp.concatenate([tall_ref[tile:, :], high[terms - tile :]], axis=0)
    scores = jnp.dot(rows, tall_ref[:tile, :], preferred_element_type=jnp.float32)
    bias = sum(jnp.dot(marks, piece, preferred_element_type=jnp.float32) for piece in rest)
    scores = scores + (jnp.dot(marks, high, preferred_element_type=jnp.float32) + bias)
    peak = jnp.max(scores, axis=1, keepdims=True)
    weight = jnp.sum(jnp.exp(scores - peak), axis=1, keepdims=True)
    scores_ref[...] = scores
    lane = lax.broadcasted_iota(jnp.int32, stats_ref.shape, 1)
    stats_ref[...] = jnp.where(lane == 0, peak, weight)


def posterior_kernel(count, rows_here, *refs):
    scores_ref = refs[0]
    stats_refs = refs[1 : 1 + count]
    posterior_ref, evidence_ref = refs[1 + count :]
    for place in range(count):
        mine = pl.ds(place * rows_here, rows_here)
        peak = stats_refs[0][mine, 0:1]
        weight = stats_refs[0][mine, 1:2]
        for step in range(1, count):
            theirs = pl.ds((place - step) % count * rows_here, rows_here)
            other_peak = stats_refs[step][theirs, 0:1]
            other_weight = stats_refs[step][theirs, 1:2]
            top = jnp.maximum(peak, other_peak)
            weight = weight * jnp.exp(peak - top) + other_weight * jnp.exp(other_peak - top)
            peak = top
        evidence = peak + jnp.log(weight)
        posterior_ref[mine, :] = jnp.exp(scores_ref[mine, :] - evidence).astype(jnp.bfloat16)
        if place == 0:
            evidence_ref[...] = jnp.broadcast_to(evidence, evidence_ref.shape)


def sums_kernel(team, count, *refs):
    weight_refs, slab_refs, out_ref = refs[:team], refs[team:-1], refs[-1]
    rows_here = weight_refs[0].shape[0] // count
    width = out_ref.shape[1]
    weights = [
        ref[pl.ds(place * rows_here, rows_here), :]
        for place in range(count)
        for ref in weight_refs
    ]
    member = lax.rem(lax.axis_index("img"), team)
    slabs = []
    for place, ref in enumerate(slab_refs):
        if place and place % team == 0:
            slabs.append(ref[:, pl.ds(pl.multiple_of(member * width, LANES), width)])
        else:
            slabs.append(ref[...])
    out_ref[...] = first_rows(
        jnp.concatenate(weights, axis=0), jnp.concatenate(slabs, axis=0)
    ).astype(out_ref.dtype)


def body(images, projections, noise_power, class_logprior, groups, offsets):
    rows_here, terms = images.shape
    proj_here = projections.shape[0]
    cycle_size = lax.axis_size("cls")
    owners = lax.axis_size("img")
    team = group_of(owners)
    group_count = noise_power.shape[0]
    class_count = class_logprior.shape[0]
    tags = group_count + class_count
    tag_column = terms if terms % LANES + tags <= LANES else -(-terms // LANES) * LANES
    width = -(-(tag_column + tags) // (LANES * team)) * LANES
    per_class = proj_here * cycle_size // class_count
    all_rows = cycle_size * rows_here
    grant = functools.partial(pltpu.CompilerParams, vmem_limit_bytes=GRANT)
    scalars = pl.BlockSpec(memory_space=pltpu.SMEM)
    local = pl.BlockSpec(memory_space=pltpu.VMEM)

    remote = pl.BlockSpec(memory_space=pltpu.HBM)

    whitened, narrow, tall, *parts = pl.pallas_call(
        functools.partial(whiten_kernel, team, tag_column, class_count),
        out_shape=(
            jax.ShapeDtypeStruct((rows_here, team * width), jnp.bfloat16),
            jax.ShapeDtypeStruct((2 * group_count, terms), jnp.bfloat16),
            jax.ShapeDtypeStruct((terms, proj_here), jnp.bfloat16),
        )
        + (jax.ShapeDtypeStruct((rows_here, width), jnp.bfloat16),) * team,
        in_specs=[remote] * 5,
        out_specs=(local,) * (3 + team),
        scratch_shapes=[
            pltpu.VMEM((1, rows_here), jnp.int32),
            pltpu.VMEM((1, rows_here), jnp.int32),
            pltpu.VMEM((rows_here, terms), jnp.bfloat16),
            pltpu.VMEM((group_count, terms), jnp.float32),
            pltpu.SemaphoreType.DMA((2,)),
            pltpu.SemaphoreType.DMA((team,)),
            pltpu.SemaphoreType.DMA((team,)),
            pltpu.SemaphoreType.DMA,
        ],
        compiler_params=grant(),
        cost_estimate=pl.CostEstimate(
            flops=2 * rows_here * PARTS * group_count * terms,
            bytes_accessed=4 * rows_here * terms + 4 * group_count * terms,
            transcendentals=0,
        ),
        name="whiten",
    )(
        *(
            pltpu.with_memory_space_constraint(value, pltpu.HBM)
            for value in (
                groups.reshape(1, rows_here),
                offsets.reshape(1, rows_here),
                images,
                noise_power,
                projections.T,
            )
        ),
    )

    table = pl.pallas_call(
        functools.partial(table_kernel, tag_column % LANES, per_class),
        out_shape=jax.ShapeDtypeStruct((LANES, proj_here), jnp.float32),
        in_specs=[scalars, local, local],
        out_specs=local,
        cost_estimate=pl.CostEstimate(
            flops=8 * proj_here * group_count * terms,
            bytes_accessed=2 * proj_here * terms + 4 * group_count * terms,
            transcendentals=0,
        ),
        compiler_params=grant(),
        name="table",
    )(class_logprior, narrow, tall)

    gathered = gathered_from(whitened, "cls")
    swapped = [parts[0]] + [crossed(parts[flip], "img", flip) for flip in range(1, team)]

    scores, stats = pl.pallas_call(
        functools.partial(score_kernel, tag_column, cycle_size),
        out_shape=(
            jax.ShapeDtypeStruct((all_rows, proj_here), jnp.float32),
            jax.ShapeDtypeStruct((all_rows, LANES), jnp.float32),
        ),
        in_specs=[local] * (cycle_size + 2),
        out_specs=(local, local),
        cost_estimate=pl.CostEstimate(
            flops=2 * all_rows * proj_here * terms,
            bytes_accessed=2 * (all_rows + proj_here) * terms,
            transcendentals=all_rows * proj_here,
        ),
        compiler_params=grant(),
        name="scores",
    )(*gathered, tall, table)

    posterior, evidence = pl.pallas_call(
        functools.partial(posterior_kernel, cycle_size, rows_here),
        out_shape=(
            jax.ShapeDtypeStruct((all_rows, proj_here), jnp.bfloat16),
            jax.ShapeDtypeStruct((rows_here, LANES), jnp.float32),
        ),
        in_specs=[local] * (cycle_size + 1),
        out_specs=(local, local),
        compiler_params=grant(),
        name="posterior",
    )(scores, *gathered_from(stats, "cls"))

    weights = [posterior]
    for flip in range(1, team):
        weights.append(crossed(posterior, "img", flip))
    slabs = list(swapped)
    for step in range(1, cycle_size):
        slabs.append(gathered[step])
        for flip in range(1, team):
            slabs.append(shifted(swapped[flip], "cls", step))
    sums = pl.pallas_call(
        functools.partial(sums_kernel, team, cycle_size),
        out_shape=jax.ShapeDtypeStruct((proj_here, width), jnp.bfloat16),
        in_specs=[local] * (team + team * cycle_size),
        out_specs=local,
        cost_estimate=pl.CostEstimate(
            flops=2 * team * all_rows * proj_here * width,
            bytes_accessed=2 * (team * all_rows + proj_here) * width,
            transcendentals=0,
        ),
        compiler_params=grant(),
        name="sums",
    )(*weights, *slabs)
    blocks = sums.reshape(owners, proj_here // owners, width)
    pieces = lax.all_to_all(blocks, "img", 0, 0)
    pieces = pieces.reshape(owners // team, team, proj_here // owners, width)
    total = jnp.sum(pieces.astype(jnp.float32), axis=0)
    sum_rows = jnp.concatenate([total[place] for place in range(team)], axis=1)[:, :terms]
    return (sum_rows, evidence[:, 0])


def solution(mesh):
    in_specs = (
        P(("cls", "img"), None),
        P("cls", None),
        P(),
        P(),
        P(("cls", "img")),
        P(("cls", "img")),
    )
    out_specs = (P(("cls", "img"), None), P(("cls", "img")))
    return jax.shard_map(body, mesh=mesh, in_specs=in_specs, out_specs=out_specs, check_vma=False)
```
